32 devices in a mesh: groups: 2 (over x), row: 16 (over z, y, core).
Axes of the slice: x: 2, y: 2, z: 4, core: 2. Of those that a mesh axis runs over, the one named last changes fastest.
Arguments:
- exterior_map: bfloat16 [15360, 7680], P(('groups', 'row')), parts along dimension 0, may hold values from -6 to 6
- couple_maps: bfloat16 [4, 7680, 1024], P('groups', 'row'), parts along dimension 0, may hold values from -0.1875 to 0.1875
- face_from_exterior: bfloat16 [15360, 1024], P(('groups', 'row')), parts along dimension 0, may hold values from -12 to 12
- face_maps: float32 [4096, 1024], P(('groups', 'row')), parts along dimension 0, may hold values from -1 to 2
- start_inverse: float32 [2048, 1024], P('groups'), parts along dimension 0, may hold values from -1 to 1
Outputs:
- merged_columns: bfloat16 [2, 15360, 7680], P(None, ('groups', 'row')), parts along dimension 1
The draws below stay inside these ranges and needn't reach their ends.
There are 2 independent parts, one for each index of `groups`. The reference program is written for one: setup_inputs(seed, part) draws one part's arguments, and reference() takes and returns one part's arrays. A program takes and returns all parts, laid end to end along the dimension named above; each array names one. Nothing has to cross between parts.
All inputs are finite; a program needn't handle non-finite values.
Results may differ from the reference program's by a relative error of at most 0.0095.
Values may be sent and summed in bfloat16 or wider, within the bound.
No kernel may reach another device: no remote copies, remote signals or barrier semaphores. Data moves between devices by JAX's collectives and lax.ppermute only.
A program may use at most 128 MiB of HBM per device.

```python
import math
import jax
import jax.numpy as jnp
from jax import lax

E = 7680
S = 1024
NEWTON = 2


def face_parts(key):
    base = jax.random.fold_in(key, 7001)
    keys = jax.random.split(base, 5)
    diag_first = jax.random.uniform(keys[0], (S,), jnp.float32, 1.0, 1.5)
    diag_second = jax.random.uniform(keys[1], (S,), jnp.float32, 1.0, 1.5)
    noise_first = jnp.clip(jax.random.normal(keys[2], (S, S), jnp.float32), -4.0, 4.0)
    noise_second = jnp.clip(jax.random.normal(keys[3], (S, S), jnp.float32), -4.0, 4.0)
    extra = jnp.clip(jax.random.normal(keys[4], (S, S), jnp.float32), -4.0, 4.0)
    scale_root = 1.0 / math.sqrt(S)
    face_first = jnp.diag(diag_first) + 0.71 * scale_root * noise_first
    face_second = jnp.diag(diag_second) + 0.71 * scale_root * noise_second
    recip = 1.0 / (diag_first + diag_second)
    inverse = jnp.diag(recip) - recip[:, None] * (1.2 * scale_root * extra) * recip[None, :]
    return (face_first, face_second, inverse)


def draw_face_maps(key, part):
    face_first, face_second, inverse = face_parts(key)
    return jnp.concatenate([face_first, face_second], axis=0)


def draw_start_inverse(key, part):
    face_first, face_second, inverse = face_parts(key)
    return inverse


def block_levels(own_key, dims, shards, low, top_value):
    loudness = 1.0
    for dim, blocks in shards:
        draws = jax.random.uniform(jax.random.fold_in(jax.random.fold_in(own_key, 6), dim), (blocks,), jnp.float32, low / len(shards), top_value / len(shards))
        loudness = loudness * jnp.repeat(jnp.exp(draws), dims[dim] // blocks).reshape((-1,) + (1,) * (len(dims) - 1 - dim))
    return loudness


def bell_draw(own_key, shape, width, reach, cuts=(), dtype=jnp.bfloat16):
    array = jax.random.normal(own_key, shape, jnp.float32) * width
    if len(cuts) > 0:
        array = block_levels(own_key, shape, cuts, -0.22, 0.18) * array
    return jnp.clip(array, min=-reach, max=reach).astype(dtype)


def setup_inputs(seed: int = 0, part: int = 0) -> dict:
    streams_of = jax.random.split(jax.random.key(seed), 6)
    part_keys = jax.random.split(jax.random.fold_in(streams_of[5], part), 6)
    exterior_map = bell_draw(part_keys[0], (E, E), 1.0, 6.0, ((0, 16),))
    couple_maps = bell_draw(part_keys[1], (2, E, S), S ** -0.5, 0.1875, ((1, 16),))
    face_from_exterior = bell_draw(part_keys[2], (E, S), 3.0, 12.0, ((0, 16),))
    face_maps = draw_face_maps(jax.random.fold_in(jax.random.fold_in(streams_of[5], part), 71), part)
    start_inverse = draw_start_inverse(jax.random.fold_in(jax.random.fold_in(streams_of[5], part), 71), part)
    return dict(exterior_map=exterior_map, couple_maps=couple_maps, face_from_exterior=face_from_exterior, face_maps=face_maps, start_inverse=start_inverse)


def reference(exterior_map, couple_maps, face_from_exterior, face_maps, start_inverse):
    high = lax.Precision.HIGHEST
    coupling = face_maps[:S] + face_maps[S:]
    iterate = start_inverse
    for newton_step in range(NEWTON):
        product = jnp.dot(coupling, iterate, precision=high, preferred_element_type=jnp.float32)
        iterate = 2.0 * iterate - jnp.dot(iterate, product, precision=high, preferred_element_type=jnp.float32)
    panel_rows = face_from_exterior.astype(jnp.float32)
    face_image = jnp.dot(iterate, panel_rows.T, precision=high, preferred_element_type=jnp.float32).astype(jnp.bfloat16)
    upper = jnp.dot(couple_maps[0], face_image, preferred_element_type=jnp.float32)
    lower = jnp.dot(couple_maps[1], face_image, preferred_element_type=jnp.float32)
    merged_upper = (exterior_map.astype(jnp.float32) - upper).astype(jnp.bfloat16)
    merged_lower = (-lower).astype(jnp.bfloat16)
    return jnp.stack([merged_upper, merged_lower])
```

```python
import functools
import math

import jax
import jax.numpy as jnp
from jax import lax
from jax.experimental import pallas as pl
from jax.experimental.pallas import tpu as pltpu
from jax.sharding import PartitionSpec as P

NT = (((1,), (1,)), ((), ()))
BF16 = jnp.bfloat16
F32 = jnp.float32


def ring_order(chips):
    return list(range(0, chips, 2)) + list(range(chips - 1, 0, -2))


def ring_chip(place, chips):
    place = lax.rem(place + 2 * chips, chips)
    return jnp.where(place < chips // 2, 2 * place, 2 * (chips - 1 - place) + 1)


def ring_place(chip, chips):
    return jnp.where(chip % 2 == 0, chip // 2, chips - 1 - (chip - 1) // 2)


def chain_kernel(rows, tab, base, *refs):
    pieces = refs[:-5]
    out, full, wide, narrow, sem = refs[-5:]
    loads = [
        pltpu.make_async_copy(
            piece.at[pl.ds(k * rows, rows), :],
            full.at[pl.ds(pl.multiple_of(tab[2 * i + k], rows), rows), :],
            sem.at[2 * i + k],
        )
        for i, piece in enumerate(pieces)
        for k in range(2)
    ]
    for load in loads:
        load.start()
    narrow[0] = base[...].astype(BF16)
    for load in loads:
        load.wait()
    size = full.shape[1]
    tile = math.gcd(size, 256)
    cols = lambda j: pl.ds(pl.multiple_of(j * tile, tile), tile)

    @pl.loop(0, size // tile)
    def _(j):
        first = base[:, cols(j)] + jnp.dot(
            narrow[0], full[:, cols(j)], preferred_element_type=F32
        )
        wide[:, cols(j)] = first
        narrow[1, :, cols(j)] = first.astype(BF16)

    @pl.loop(0, size // tile)
    def _(j):
        narrow[0, :, cols(j)] = jnp.dot(
            narrow[1], full[:, cols(j)], preferred_element_type=F32
        ).astype(BF16)

    @pl.loop(0, size // tile)
    def _(j):
        out[:, cols(j)] = (
            wide[:, cols(j)]
            + jnp.dot(narrow[0], full[:, cols(j)], preferred_element_type=F32)
        ).astype(BF16)


def chain(tab, base, pieces, rows):
    m, size = base.shape
    vmem = pl.BlockSpec(memory_space=pltpu.VMEM)
    return pl.pallas_call(
        functools.partial(chain_kernel, rows),
        out_shape=jax.ShapeDtypeStruct((m, size), BF16),
        in_specs=[pl.BlockSpec(memory_space=pltpu.SMEM), vmem]
        + [pl.BlockSpec(memory_space=pl.ANY)] * len(pieces),
        out_specs=vmem,
        scratch_shapes=[
            pltpu.VMEM((size, size), BF16),
            pltpu.VMEM((m, size), F32),
            pltpu.VMEM((2, m, size), BF16),
            pltpu.SemaphoreType.DMA((2 * len(pieces),)),
        ],
        compiler_params=pltpu.CompilerParams(vmem_limit_bytes=36 * 2**20),
        cost_estimate=pl.CostEstimate(
            flops=6 * m * size * size, bytes_accessed=8 * m * size, transcendentals=0
        ),
        name="chain",
    )(tab, base, *pieces)


def stage_kernel(count, windows, olds, tab, *refs):
    refs = list(refs)
    take = lambda n: [refs.pop(0) for _ in range(n)]
    pieces = take(count)
    mixed, own = take(2) if windows else (None, None)
    take(olds)
    (full,) = take(1)
    (out,) = take(1) if windows else (None,)
    if count:
        bounce, in_sem, out_sem = take(3)
        rows = pieces[0].shape[0]
        ins = [
            pltpu.make_async_copy(pieces[i], bounce.at[i], in_sem.at[i])
            for i in range(count)
        ]
        outs = [
            pltpu.make_async_copy(
                bounce.at[i],
                full.at[pl.ds(pl.multiple_of(tab[i], 16), rows), :],
                out_sem.at[i],
            )
            for i in range(count)
        ]
        for copy in ins:
            copy.start()
        for i in range(count):
            ins[i].wait()
            outs[i].start()
        for copy in outs:
            copy.wait()
    if not windows:
        return
    panel, held, done, load_sem, store_sem = take(5)
    width = panel.shape[1]
    tile = math.gcd(width, 256)

    def cols(i):
        return pl.ds(pl.multiple_of(tab[count + i], 128), width)

    def loads(i, slot):
        return (
            pltpu.make_async_copy(
                full.at[cols(i), :], panel.at[slot], load_sem.at[0, slot]
            ),
            pltpu.make_async_copy(
                own.at[:, cols(i)], held.at[slot], load_sem.at[1, slot]
            ),
        )

    def store(i, slot):
        return pltpu.make_async_copy(
            done.at[slot], out.at[:, :, cols(i)], store_sem.at[slot]
        )

    for copy in loads(0, 0):
        copy.start()

    @pl.loop(0, windows)
    def _(i):
        slot = lax.rem(i, 2)

        @pl.when(i + 1 < windows)
        def _():
            for copy in loads(i + 1, 1 - slot):
                copy.start()

        for copy in loads(i, slot):
            copy.wait()

        for j in range(width // tile):
            span = pl.ds(j * tile, tile)
            part = panel[slot, span, :]
            upper = lax.dot_general(mixed[0], part, NT, preferred_element_type=F32)
            done[slot, 0, :, span] = (
                held[slot, :, span].astype(F32) - upper
            ).astype(BF16)
            lower = lax.dot_general(mixed[1], part, NT, preferred_element_type=F32)
            done[slot, 1, :, span] = (-lower).astype(BF16)

        @pl.when(i > 0)
        def _():
            store(i - 1, 1 - slot).wait()

        store(i, slot).start()

    store(windows - 1, (windows - 1) % 2).wait()


def stage(tab, pieces, full, mixed=None, own=None, out=None, windows=0, width=0, total=0):
    count = len(pieces)
    hbm = pl.BlockSpec(memory_space=pl.ANY)
    args = [tab, *pieces]
    in_specs = [pl.BlockSpec(memory_space=pltpu.SMEM)] + [hbm] * count
    shapes = [jax.ShapeDtypeStruct((total, pieces[0].shape[1]), BF16)] if full is None else [
        jax.ShapeDtypeStruct(full.shape, BF16)
    ]
    size = shapes[0].shape[1]
    scratch = []
    if count:
        scratch += [
            pltpu.VMEM((count, *pieces[0].shape), BF16),
            pltpu.SemaphoreType.DMA((count,)),
            pltpu.SemaphoreType.DMA((count,)),
        ]
    if windows:
        maps, mine = mixed.shape[:2]
        args += [mixed, own]
        in_specs += [pl.BlockSpec(memory_space=pltpu.VMEM), hbm]
        shapes.append(jax.ShapeDtypeStruct((maps, mine, own.shape[1]), BF16))
        scratch += [
            pltpu.VMEM((2, width, size), BF16),
            pltpu.VMEM((2, mine, width), BF16),
            pltpu.VMEM((2, maps, mine, width), BF16),
            pltpu.SemaphoreType.DMA((2, 2)),
            pltpu.SemaphoreType.DMA((2,)),
        ]
    olds = [(old, k) for k, old in enumerate((full, out)) if old is not None]
    aliases = {len(args) + i: k for i, (_, k) in enumerate(olds)}
    args += [old for old, _ in olds]
    in_specs += [hbm] * len(olds)
    flops = windows * 4 * (mixed.shape[1] if windows else 0) * size * width
    moved = 4 * sum(p.size for p in pieces) + windows * width * (size + 3 * size) * 2
    return pl.pallas_call(
        functools.partial(stage_kernel, count, windows, len(olds)),
        out_shape=shapes,
        in_specs=in_specs,
        out_specs=[hbm] * len(shapes),
        scratch_shapes=scratch,
        input_output_aliases=aliases,
        compiler_params=pltpu.CompilerParams(vmem_limit_bytes=24 * 2**20),
        cost_estimate=pl.CostEstimate(
            flops=flops, bytes_accessed=moved, transcendentals=0
        ),
        name="stage",
    )(*args)


def per_device(exterior_map, couple_maps, face_from_exterior, face_maps, start_inverse):
    high = lax.Precision.HIGHEST
    devices = lax.axis_size("row")
    chips = devices // 2
    half = chips // 2
    me = lax.axis_index("row")
    chip, core = me // 2, me % 2
    place = ring_place(chip, chips)
    size = start_inverse.shape[0]
    order = ring_order(chips)

    ring_pairs = []
    for i in range(chips):
        ring_pairs.append((2 * order[i], 2 * order[(i + 1) % chips]))
        ring_pairs.append((2 * order[i] + 1, 2 * order[i - 1] + 1))
    hop = lambda block: lax.ppermute(block, "row", ring_pairs)
    swap = lambda block: lax.ppermute(block, "row", [(i, i ^ 1) for i in range(devices)])
    far = lambda block: lax.ppermute(
        block, "row", [(i, (i + chips) % devices) for i in range(devices)]
    )

    face_rows = face_maps.shape[0] // 2
    side = me // chips
    keep = lax.dynamic_slice_in_dim(face_maps, side * face_rows, face_rows, 0)
    give = lax.dynamic_slice_in_dim(face_maps, (1 - side) * face_rows, face_rows, 0)
    coupling = keep + far(give.astype(BF16)).astype(F32)

    def residual_start(device):
        return 2 * face_rows * (device % chips) + face_rows * (device // chips)

    eye = (
        lax.broadcasted_iota(jnp.int32, (face_rows, size), 1)
        == lax.broadcasted_iota(jnp.int32, (face_rows, size), 0) + residual_start(me)
    ).astype(F32)
    residual = (
        eye - jnp.dot(coupling, start_inverse, precision=high, preferred_element_type=F32)
    ).astype(BF16)

    away = jnp.where(core == 0, -1, 1)

    def shard_at(steps, own_core):
        return 2 * ring_chip(place + steps, chips) + own_core

    pair = jnp.concatenate([residual, swap(residual)], axis=0)
    residual_pieces = [pair]
    residual_shards = [me, me ^ 1]
    block = pair
    for step in range(1, half + 1):
        block = hop(block)
        residual_pieces.append(block)
        residual_shards += [
            shard_at(away * step, core),
            shard_at(away * step, 1 - core),
        ]
        if step < half:
            residual_pieces.append(swap(block))
            residual_shards += [
                shard_at(-away * step, 1 - core),
                shard_at(-away * step, core),
            ]

    rows = face_from_exterior.shape[0]
    first, second = face_from_exterior, swap(face_from_exterior)
    groups = [([first, second], [me, me ^ 1], [chip])]
    for step in range(1, half + 1):
        blocks, shards = [], []
        first = hop(first)
        blocks += [first, swap(first)]
        shards += [shard_at(away * step, core), shard_at(-away * step, 1 - core)]
        if step < half:
            second = hop(second)
            blocks += [second, swap(second)]
            shards += [shard_at(away * step, 1 - core), shard_at(-away * step, core)]
            both = [ring_chip(place + step, chips), ring_chip(place - step, chips)]
        else:
            both = [ring_chip(place + step, chips)]
        groups.append((blocks, shards, both))

    maps, mine = couple_maps.shape[:2]
    left = couple_maps.reshape(maps * mine, size)
    upper_part = lax.reduce_precision(start_inverse, 8, 7)
    lower_part = (start_inverse - upper_part).astype(BF16)
    base = jnp.dot(left, upper_part.astype(BF16), preferred_element_type=F32) + jnp.dot(
        left, lower_part, preferred_element_type=F32
    )
    starts = jnp.stack([residual_start(d) for d in residual_shards]).astype(jnp.int32)
    mixed = chain(starts, base, residual_pieces, face_rows).reshape(maps, mine, size)

    span = 2 * rows
    total = devices * rows
    width = -(-(span + 128 - math.gcd(span, 128)) // 128) * 128

    def table(shards, chips_done):
        starts = [shard * rows for shard in shards] + [
            jnp.minimum(c * span // 128 * 128, total - width) for c in chips_done
        ]
        return jnp.stack(starts).astype(jnp.int32)

    full = out = None
    early = []
    for step, (blocks, shards, done) in enumerate(groups):
        if step < half - 1:
            (full,) = stage(table(shards, []), blocks, full, total=total)
            early += done
        else:
            if step == half - 1:
                full, out = stage(
                    table([], early), [], full, mixed, exterior_map, out, len(early), width
                )
            full, out = stage(
                table(shards, done), blocks, full, mixed, exterior_map, out, len(done), width
            )
    return out


def solution(mesh):
    return jax.shard_map(
        per_device,
        mesh=mesh,
        in_specs=(
            P(("groups", "row"), None),
            P("groups", "row", None),
            P(("groups", "row"), None),
            P(("groups", "row"), None),
            P("groups", None),
        ),
        out_specs=P(None, ("groups", "row"), None),
        check_vma=False,
    )
```
